256 devices in a mesh: peer: 32 (over z, y_hi, core), grp: 8 (over y_lo, x).
Axes of the slice: x: 4, y: 4 (y_hi: 2, y_lo: 2; y = y_hi * 2 + y_lo), z: 8, core: 2. Of those that a mesh axis runs over, the one named last changes fastest.
Arguments:
- images: bfloat16 [2, 32, 8, 8, 32, 384], P(None, 'peer', 'grp'), may hold values from -6 to 6
- cotangent: bfloat16 [2, 32, 8, 8, 32, 384], P(None, 'peer', 'grp'), may hold values from -6 to 6
- dw_kernel: float32 [32, 49, 384], P('peer', None, 'grp'), may hold values from -0.875 to 0.875
- chan_vec: float32 [32, 5, 384], P('peer', None, 'grp'), may hold values from 0.25 to 1.5
- w_in: float32 [32, 384, 1536], P('peer', 'grp'), may hold values from -0.3125 to 0.3125
- b_in: float32 [32, 1536], P('peer', 'grp'), may hold values from -3 to 3
- w_out: float32 [32, 1536, 384], P('peer', 'grp'), may hold values from -0.15625 to 0.15625
- mom_kernel: float32 [32, 49, 384], P('peer', None, 'grp'), may hold values from -300 to 300
- mom_chan: float32 [32, 5, 384], P('peer', None, 'grp'), may hold values from -300 to 300
- mom_in: float32 [32, 384, 1536], P('peer', 'grp'), may hold values from -300 to 300
- mom_bin: float32 [32, 1536], P('peer', 'grp'), may hold values from -300 to 300
- mom_out: float32 [32, 1536, 384], P('peer', 'grp'), may hold values from -300 to 300
Outputs:
- new_kernel: float32 [32, 49, 384], P('peer', None, 'grp')
- new_chan: float32 [32, 5, 384], P('peer', None, 'grp')
- new_in: float32 [32, 384, 1536], P('peer', 'grp')
- new_bin: float32 [32, 1536], P('peer', 'grp')
- new_out: float32 [32, 1536, 384], P('peer', 'grp')
- features: bfloat16 [32, 8, 8, 32, 384], P('peer', 'grp')
The draws below stay inside these ranges and needn't reach their ends.
All inputs are finite; a program needn't handle non-finite values.
Results may differ from the reference program's by a relative error of at most 0.01.
Values may be sent and summed in bfloat16 or wider, within the bound.
No kernel may reach another device: no remote copies, remote signals or barrier semaphores. Data moves between devices by JAX's collectives and lax.ppermute only.
A program may use at most 64 MiB of HBM per device.

```python
import math
import jax
import jax.numpy as jnp
from jax import lax

CHANNELS = 384
HIDDEN_SIZE = 1536
HEIGHT = 8
WIDTH = 32
TAPS = 49
STEPS = 2
REPLICAS = 32
GROUPS = 8


def block_scale(key, shape, shards, low, high):
    def one(axis_at, blocks):
        steps = jax.random.uniform(jax.random.fold_in(jax.random.fold_in(key, 6), axis_at), (blocks,), jnp.float32, low / len(shards), high / len(shards))
        return jnp.repeat(jnp.exp(steps), shape[axis_at] // blocks).reshape((-1,) + (1,) * (len(shape) - axis_at - 1))

    loudness = one(*shards[0])
    for cut in shards[1:]:
        loudness = loudness * one(*cut)
    return loudness


def centred(rng, dims, scale, most, cuts=(), held_as=jnp.bfloat16):
    result = jax.random.normal(rng, dims, jnp.float32) * scale
    if len(cuts) > 0:
        result = block_scale(rng, dims, cuts, -0.22, 0.18) * result
    return jnp.clip(result, min=-most, max=most).astype(held_as)


def setup_inputs(seed: int = 0) -> dict:
    arg_keys = jax.random.split(jax.random.key(seed), 13)
    return {
        "images": centred(arg_keys[0], (STEPS, REPLICAS, GROUPS, HEIGHT, WIDTH, CHANNELS), 1.0, 6.0, ((1, 32), (2, 8))),
        "cotangent": centred(arg_keys[1], (STEPS, REPLICAS, GROUPS, HEIGHT, WIDTH, CHANNELS), 1.0, 6.0, ((1, 32), (2, 8))),
        "dw_kernel": centred(arg_keys[2], (REPLICAS, TAPS, CHANNELS), TAPS ** -0.5, 0.875, ((0, 32), (2, 8)), jnp.float32),
        "chan_vec": jnp.clip(0.25 + 1.25 * jax.random.uniform(arg_keys[3], (REPLICAS, 5, CHANNELS), jnp.float32) ** block_scale(arg_keys[3], (REPLICAS, 5, CHANNELS), ((0, 32), (2, 8)), -0.2, 0.2), 0.25, 1.5),
        "w_in": centred(arg_keys[4], (REPLICAS, CHANNELS, HIDDEN_SIZE), CHANNELS ** -0.5, 0.3125, ((0, 32), (1, 8)), jnp.float32),
        "b_in": centred(arg_keys[5], (REPLICAS, HIDDEN_SIZE), 0.5, 3.0, ((0, 32), (1, 8)), jnp.float32),
        "w_out": centred(arg_keys[6], (REPLICAS, HIDDEN_SIZE, CHANNELS), HIDDEN_SIZE ** -0.5, 0.15625, ((0, 32), (1, 8)), jnp.float32),
        "mom_kernel": centred(arg_keys[7], (REPLICAS, TAPS, CHANNELS), 50.0, 300.0, ((0, 32), (2, 8)), jnp.float32),
        "mom_chan": centred(arg_keys[8], (REPLICAS, 5, CHANNELS), 50.0, 300.0, ((0, 32), (2, 8)), jnp.float32),
        "mom_in": centred(arg_keys[9], (REPLICAS, CHANNELS, HIDDEN_SIZE), 50.0, 300.0, ((0, 32), (1, 8)), jnp.float32),
        "mom_bin": centred(arg_keys[10], (REPLICAS, HIDDEN_SIZE), 50.0, 300.0, ((0, 32), (1, 8)), jnp.float32),
        "mom_out": centred(arg_keys[11], (REPLICAS, HIDDEN_SIZE, CHANNELS), 50.0, 300.0, ((0, 32), (1, 8)), jnp.float32),
    }


EPS = 1e-06
MOMENTUM = 0.9
RATE = 0.0005
SQRT_HALF = 0.7071067811865476
INV_ROOT_TWO_PI = 0.3989422804014327

def depthwise(field, kernel):
    channels = kernel.shape[-1]
    reach = math.isqrt(kernel.shape[0])
    margin = reach // 2
    filter_taps = kernel.reshape(reach, reach, 1, channels)
    return lax.conv_general_dilated(field, filter_taps, (1, 1), ((margin, margin), (margin, margin)), dimension_numbers=('NHWC', 'HWIO', 'NHWC'), feature_group_count=channels, precision=lax.Precision.HIGHEST)

def gelu_value(value):
    return 0.5 * value * (1.0 + lax.erf(value * SQRT_HALF))

def gelu_slope(value):
    return 0.5 * (1.0 + lax.erf(value * SQRT_HALF)) + value * jnp.exp(-0.5 * value * value) * INV_ROOT_TWO_PI

def channel_front(image, kernel, chan):
    height, width, channels = image.shape
    field = image.astype(jnp.float32)[None]
    conv = depthwise(field, kernel)[0].reshape(height * width, channels) + chan[0]
    center = conv - lax.optimization_barrier(jnp.mean(conv, axis=-1, keepdims=True))
    spread = lax.rsqrt(lax.optimization_barrier(jnp.mean(center * center, axis=-1, keepdims=True)) + EPS)
    scaled = center * spread
    normed = (scaled * chan[1] + chan[2]).astype(jnp.bfloat16)
    return (field, scaled, spread, normed)

def channel_back(field, scaled, spread, dnormed, chan, kernel, bias_grad, scale_grad):
    d_gain = lax.optimization_barrier(jnp.sum(dnormed * scaled, axis=0))
    d_shift = lax.optimization_barrier(jnp.sum(dnormed, axis=0))
    dscaled = dnormed * chan[1]
    dconv = spread * (dscaled - lax.optimization_barrier(jnp.mean(dscaled, axis=-1, keepdims=True)) - scaled * lax.optimization_barrier(jnp.mean(dscaled * scaled, axis=-1, keepdims=True)))
    d_bias = lax.optimization_barrier(jnp.sum(dconv, axis=0))
    _, pullback = jax.vjp(lambda taps: depthwise(field, taps), kernel)
    d_kernel, = pullback(dconv.reshape(field.shape))
    d_chan = jnp.stack([d_bias, d_gain, d_shift, bias_grad, scale_grad])
    return (d_kernel, d_chan)

def local_pass(image, cot_image, kernel, chan, w_in, b_in, w_out):
    height, width, channels = image.shape
    rows = height * width
    w_in_low = w_in.astype(jnp.bfloat16)
    w_out_low = w_out.astype(jnp.bfloat16)
    field, scaled, spread, normed = channel_front(image, kernel, chan)
    pre = jnp.dot(normed, w_in_low, preferred_element_type=jnp.float32) + b_in
    hidden = gelu_value(pre).astype(jnp.bfloat16)
    mlp = jnp.dot(hidden, w_out_low, preferred_element_type=jnp.float32) + chan[3]
    output = (image.reshape(rows, channels).astype(jnp.float32) + chan[4] * mlp).astype(jnp.bfloat16)
    cot = cot_image.reshape(rows, channels).astype(jnp.float32)
    bias_grad = lax.optimization_barrier(jnp.sum(cot * chan[4], axis=0))
    scale_grad = lax.optimization_barrier(jnp.sum(cot * mlp, axis=0))
    dmlp = (cot * chan[4]).astype(jnp.bfloat16)
    g_out = jnp.dot(hidden.T, dmlp, preferred_element_type=jnp.float32)
    dhid = jnp.dot(dmlp, w_out_low.T, preferred_element_type=jnp.float32)
    dpre = (dhid * gelu_slope(pre)).astype(jnp.bfloat16)
    g_bin = lax.optimization_barrier(jnp.sum(dpre.astype(jnp.float32), axis=0))
    g_in = jnp.dot(normed.T, dpre, preferred_element_type=jnp.float32)
    dnormed = jnp.dot(dpre, w_in_low.T, preferred_element_type=jnp.float32)
    d_kernel, d_chan = channel_back(field, scaled, spread, dnormed, chan, kernel, bias_grad, scale_grad)
    return (output.reshape(height, width, channels), (d_kernel, d_chan, g_in, g_bin, g_out))

def reference(images, cotangent, dw_kernel, chan_vec, w_in, b_in, w_out, mom_kernel, mom_chan, mom_in, mom_bin, mom_out):
    params = (dw_kernel, chan_vec, w_in, b_in, w_out)
    moments = (mom_kernel, mom_chan, mom_in, mom_bin, mom_out)
    features = None
    for round_index in range(STEPS):

        def replica(packed):
            local_params, image_set, cot_set = packed
            total = None
            outputs = []
            for member in range(GROUPS):
                output, grads = local_pass(image_set[member], cot_set[member], *local_params)
                outputs.append(output)
                total = grads if total is None else tuple((a + b for a, b in zip(total, grads)))
            return (jnp.stack(outputs), total)
        features, summed = lax.map(replica, (params, images[round_index], cotangent[round_index]))
        moments = tuple((MOMENTUM * old + grad for old, grad in zip(moments, summed)))
        stepped = tuple((value - RATE * moment for value, moment in zip(params, moments)))
        distance = 2 ** round_index
        params = tuple((0.5 * (value + jnp.roll(value, distance, axis=0)) for value in stepped))
    return (params[0], params[1], params[2], params[3], params[4], features)
```

```python
import functools

import jax
import jax.numpy as jnp
from jax import lax
from jax.experimental import pallas as pl
from jax.experimental.pallas import tpu as pltpu
from jax.sharding import PartitionSpec as P

STEPS = 2
EPS = 1e-06
MOMENTUM = 0.9
RATE = 0.0005
SQRT_HALF = 0.7071067811865476
INV_ROOT_TWO_PI = 0.3989422804014327


RING = 4
PAIR = 2
HEIGHT, WIDTH, CHANNELS = 8, 32, 384
ROWS = HEIGHT * WIDTH
HIDDEN_PART = 384
BLOCK = 192
INNER = 48
TAPS = 49
PACKED = 2 * BLOCK + 16
SMALL = 56
LANES = 128

F32 = jnp.float32
BF16 = jnp.bfloat16
VMEM = pl.BlockSpec(memory_space=pltpu.VMEM)
SMEM = pl.BlockSpec(memory_space=pltpu.SMEM)


def shift(block, k):
    route = [
        (y * RING + x, y * RING + (x + k) % RING) for y in range(PAIR) for x in range(RING)
    ]
    return lax.ppermute(block, "grp", route)


def swap(block):
    route = [(y * RING + x, (1 - y) * RING + x) for y in range(PAIR) for x in range(RING)]
    return lax.ppermute(block, "grp", route)


def passed_along(block, distance):
    count = lax.axis_size("peer")
    return lax.ppermute(block, "peer", [((i - distance) % count, i) for i in range(count)])


def ring_order(slots, x):
    a, b, c, d = slots
    return lax.dynamic_slice_in_dim(jnp.stack([d, c, b, a, d, c, b]), RING - 1 - x, RING, 0)


def pair_order(own, other, y):
    return jnp.where(y == 0, jnp.stack([own, other]), jnp.stack([other, own]))


def fill_padded(refs, pad):
    for k, ref in enumerate(refs):
        rows = pl.ds(k * HEIGHT, HEIGHT)
        pad[rows, 0:8, :] = jnp.zeros((HEIGHT, 8, CHANNELS), F32)
        pad[rows, 8 : 8 + WIDTH, :] = (
            ref[0:ROWS, :].astype(F32).reshape(HEIGHT, WIDTH, CHANNELS)
        )
        pad[rows, 8 + WIDTH : 16 + WIDTH, :] = jnp.zeros((HEIGHT, 8, CHANNELS), F32)


def front_kernel(i0, i1, i2, i3, small, normed, scaled, spread, pad, conv):
    fill_padded((i0, i1, i2, i3), pad)

    def tile(t, carry):
        image = t // 3
        lanes = pl.ds(pl.multiple_of((t % 3) * LANES, LANES), LANES)
        base = image * HEIGHT
        bias = small[TAPS : TAPS + 1, lanes]
        for wt in range(WIDTH // 8):
            acc = [jnp.broadcast_to(bias, (8, LANES)) for _ in range(HEIGHT)]
            for j in range(7):
                start = 8 * wt + 5 + j
                src = [pad[base + h, start : start + 8, lanes] for h in range(HEIGHT)]
                for i in range(7):
                    tap = small[7 * i + j : 7 * i + j + 1, lanes]
                    for h in range(HEIGHT):
                        s = h + i - 3
                        if 0 <= s < HEIGHT:
                            acc[h] = acc[h] + tap * src[s]
            for h in range(HEIGHT):
                conv[(base + h) * 4 + wt, :, lanes] = acc[h]
        return carry

    lax.fori_loop(0, RING * 3, tile, 0)
    gain = small[TAPS + 1 : TAPS + 2, :]
    offset = small[TAPS + 2 : TAPS + 3, :]

    def norm(c, carry):
        v = conv[pl.ds(c * 8, 8), :, :].reshape(64, CHANNELS)
        rows = pl.ds(pl.multiple_of(c * 64, 64), 64)
        center = v - jnp.sum(v, axis=-1, keepdims=True) * (1.0 / CHANNELS)
        var = jnp.sum(center * center, axis=-1, keepdims=True) * (1.0 / CHANNELS)
        inv = lax.rsqrt(var + EPS)
        sc = center * inv
        scaled[rows, :] = sc
        spread[rows, :] = jnp.broadcast_to(inv, (64, LANES))
        normed[rows, :] = (sc * gain + offset).astype(BF16)
        return carry

    lax.fori_loop(0, RING * ROWS // 64, norm, 0)


def front(images, small):
    total = RING * ROWS
    return pl.pallas_call(
        front_kernel,
        out_shape=(
            jax.ShapeDtypeStruct((total, CHANNELS), BF16),
            jax.ShapeDtypeStruct((total, CHANNELS), F32),
            jax.ShapeDtypeStruct((total, LANES), F32),
        ),
        in_specs=[VMEM] * 5,
        out_specs=(VMEM,) * 3,
        scratch_shapes=[
            pltpu.VMEM((RING * HEIGHT, WIDTH + 16, CHANNELS), F32),
            pltpu.VMEM((RING * HEIGHT * 4, 8, CHANNELS), F32),
        ],
        name="front",
    )(*images, small)


def contract(a, b, da, db):
    return lax.dot_general(a, b, (((da,), (db,)), ((), ())), preferred_element_type=F32)


def mlp_kernel(
    last, y_ref, normed, own, other, b_ref, c0, c1, c2, c3, small, *refs
):
    g_own, g_send, dnormed, aux = refs[:4]
    partial = refs[4:8] if last else ()
    w_in, w_out, acc_out, acc_in = refs[-4:]
    y = y_ref[0]
    mine = pl.ds(pl.multiple_of(y * BLOCK, 64), BLOCK)
    theirs = pl.ds(pl.multiple_of((1 - y) * BLOCK, 64), BLOCK)
    w_out[mine, :] = own[0:BLOCK, :]
    w_out[theirs, :] = other[0:BLOCK, :]
    w_in[mine, :] = own[BLOCK : 2 * BLOCK, :]
    w_in[theirs, :] = other[BLOCK : 2 * BLOCK, :]
    bias = b_ref[...]
    b_out = small[TAPS + 3 : TAPS + 4, :]
    scale = small[TAPS + 4 : TAPS + 5, :]
    c_sum = jnp.zeros((1, CHANNELS), F32)
    g_bin = jnp.zeros((1, HIDDEN_PART), F32)
    for k, c_ref in enumerate((c0, c1, c2, c3)):
        rows = slice(k * ROWS, (k + 1) * ROWS)
        nrm = normed[rows, :]
        cot = c_ref[c_ref.shape[0] - ROWS :, :]
        wide = cot.astype(F32)
        pre = contract(nrm, w_in[...], 1, 0) + bias
        phi = 0.5 * (1.0 + lax.erf(pre * SQRT_HALF))
        hidden = (pre * phi).astype(BF16)
        slope = phi + pre * jnp.exp(-0.5 * pre * pre) * INV_ROOT_TWO_PI
        dmlp = (wide * scale).astype(BF16)
        dpre = (contract(dmlp, w_out[...], 1, 1) * slope).astype(BF16)
        dnormed[rows, :] = contract(dpre, w_in[...], 1, 1)
        go = contract(hidden, cot, 0, 0)
        gi = contract(nrm, dpre, 0, 0)
        if k == 0:
            acc_out[...] = go
            acc_in[...] = gi
        else:
            acc_out[...] += go
            acc_in[...] += gi
        c_sum = c_sum + jnp.sum(wide, axis=0, keepdims=True)
        g_bin = g_bin + jnp.sum(dpre.astype(F32), axis=0, keepdims=True)
        if last:
            partial[k][...] = contract(hidden, w_out[...], 1, 0).astype(BF16)
    share = 1.0 / RING
    scale_grad = jnp.sum(w_out[...].astype(F32) * acc_out[...], axis=0, keepdims=True)
    aux[0:1, :] = share * (scale * c_sum)
    aux[1:2, :] = scale_grad + share * (b_out * c_sum)
    g_own[0:BLOCK, :] = acc_out[mine, :] * scale
    g_send[0:BLOCK, :] = (acc_out[theirs, :] * scale).astype(BF16)
    g_own[BLOCK : 2 * BLOCK, :] = acc_in[mine, :]
    g_send[BLOCK : 2 * BLOCK, :] = acc_in[theirs, :].astype(BF16)
    first = lax.broadcasted_iota(jnp.int32, (16, HIDDEN_PART), 0) == 0
    half = (lax.broadcasted_iota(jnp.int32, (16, HIDDEN_PART), 1) >= BLOCK).astype(jnp.int32)
    block = jnp.broadcast_to(g_bin, (16, HIDDEN_PART))
    zero = jnp.zeros_like(block)
    g_own[2 * BLOCK :, :] = jnp.where(first & (half == y), block, zero)
    g_send[2 * BLOCK :, :] = jnp.where(first & (half != y), block, zero).astype(BF16)


def mlp(last, y, normed, own, other, bias, cots, small):
    total = RING * ROWS
    shapes = [
        jax.ShapeDtypeStruct((PACKED, CHANNELS), F32),
        jax.ShapeDtypeStruct((PACKED, CHANNELS), BF16),
        jax.ShapeDtypeStruct((total, CHANNELS), F32),
        jax.ShapeDtypeStruct((8, CHANNELS), F32),
    ]
    if last:
        shapes += [jax.ShapeDtypeStruct((ROWS, CHANNELS), BF16)] * RING
    return pl.pallas_call(
        functools.partial(mlp_kernel, last),
        out_shape=tuple(shapes),
        in_specs=[SMEM] + [VMEM] * 9,
        out_specs=(VMEM,) * len(shapes),
        scratch_shapes=[
            pltpu.VMEM((CHANNELS, HIDDEN_PART), BF16),
            pltpu.VMEM((HIDDEN_PART, CHANNELS), BF16),
            pltpu.VMEM((HIDDEN_PART, CHANNELS), F32),
            pltpu.VMEM((CHANNELS, HIDDEN_PART), F32),
        ],
        name="mlp",
    )(y, normed, own, other, bias, *cots, small)


def back_kernel(
    i0, i1, i2, i3, scaled, spread, dnormed, small, aux, out, pad, dconv, taps, rows_out
):
    fill_padded((i0, i1, i2, i3), pad)
    gain = small[TAPS + 1 : TAPS + 2, :]
    zero = jnp.zeros((8, CHANNELS), F32)

    def norm(c, sums):
        bias_sum, gain_sum, shift_sum = sums
        rows = pl.ds(pl.multiple_of(c * 64, 64), 64)
        sc = scaled[rows, :]
        dn = dnormed[rows, :]
        inv = spread[rows, 0:1]
        ds = dn * gain
        mean = jnp.sum(ds, axis=-1, keepdims=True) * (1.0 / CHANNELS)
        along = jnp.sum(ds * sc, axis=-1, keepdims=True) * (1.0 / CHANNELS)
        dc = (inv * (ds - mean - sc * along)).reshape(8, 8, CHANNELS)
        dconv[pl.ds(c * 8, 8), :, :] = dc
        return (
            bias_sum + jnp.sum(dc, axis=0),
            gain_sum + jnp.sum((dn * sc).reshape(8, 8, CHANNELS), axis=0),
            shift_sum + jnp.sum(dn.reshape(8, 8, CHANNELS), axis=0),
        )

    sums = lax.fori_loop(0, RING * ROWS // 64, norm, (zero, zero, zero))
    taps[...] = jnp.zeros_like(taps)

    def tile(t, carry):
        image = t // 3
        lanes = pl.ds(pl.multiple_of((t % 3) * LANES, LANES), LANES)
        base = image * HEIGHT
        for j in range(7):
            acc = [taps[7 * i + j, :, lanes] for i in range(7)]
            for wt in range(WIDTH // 8):
                start = 8 * wt + 5 + j
                src = [pad[base + h, start : start + 8, lanes] for h in range(HEIGHT)]
                grad = [dconv[(base + h) * 4 + wt, :, lanes] for h in range(HEIGHT)]
                for i in range(7):
                    for h in range(HEIGHT):
                        s = h + i - 3
                        if 0 <= s < HEIGHT:
                            acc[i] = acc[i] + grad[h] * src[s]
            for i in range(7):
                taps[7 * i + j, :, lanes] = acc[i]
        return carry

    lax.fori_loop(0, RING * 3, tile, 0)
    rows_out[0:TAPS, :] = jnp.sum(taps[...], axis=1)
    for r, value in enumerate(sums):
        rows_out[TAPS + r : TAPS + r + 1, :] = jnp.sum(value, axis=0, keepdims=True)
    rows_out[TAPS + 3 : TAPS + 5, :] = aux[0:2, :]
    rows_out[TAPS + 5 : SMALL, :] = jnp.zeros((SMALL - TAPS - 5, CHANNELS), F32)
    out[...] = rows_out[...].astype(BF16)


def back(images, scaled, spread, dnormed, small, aux):
    return pl.pallas_call(
        back_kernel,
        out_shape=jax.ShapeDtypeStruct((SMALL, CHANNELS), BF16),
        in_specs=[VMEM] * 9,
        out_specs=VMEM,
        scratch_shapes=[
            pltpu.VMEM((RING * HEIGHT, WIDTH + 16, CHANNELS), F32),
            pltpu.VMEM((RING * HEIGHT * 4, 8, CHANNELS), F32),
            pltpu.VMEM((TAPS, 8, CHANNELS), F32),
            pltpu.VMEM((SMALL, CHANNELS), F32),
        ],
        name="back",
    )(*images, scaled, spread, dnormed, small, aux)


def per_device(
    images,
    cotangent,
    dw_kernel,
    chan_vec,
    w_in,
    b_in,
    w_out,
    mom_kernel,
    mom_chan,
    mom_in,
    mom_bin,
    mom_out,
):
    member = lax.axis_index("grp")
    y, x = member // RING, member % RING
    y_scalar = y.astype(jnp.int32).reshape(1)
    photos = [images[s, 0, 0].reshape(ROWS, CHANNELS) for s in range(STEPS)]
    cots = [cotangent[s, 0, 0].reshape(ROWS, CHANNELS) for s in range(STEPS)]

    tiny = jnp.concatenate([dw_kernel[0], chan_vec[0], mom_kernel[0], mom_chan[0]], axis=0)
    couple = pair_order(tiny, swap(tiny), y)

    low = jnp.concatenate([w_in[0], mom_in[0]], axis=0).astype(BF16)

    def columns(k):
        at = ((x + k) % RING) * BLOCK
        left = lax.dynamic_slice_in_dim(low, at, BLOCK, 1)
        right = lax.dynamic_slice_in_dim(low, at + RING * BLOCK, BLOCK, 1)
        return jnp.concatenate([left, right], axis=1)

    packs = [jnp.concatenate([photos[0], columns(k)], axis=0) for k in range(RING)]
    arrived = [packs[0]] + [shift(packs[k], k) for k in range(1, RING)]
    couples = [couple] + [shift(couple, k) for k in range(1, RING)]
    whole = ring_order(couples, x)
    whole = whole.transpose(2, 1, 0, 3).reshape(2 * (TAPS + 5), CHANNELS)
    small = jnp.pad(whole[: TAPS + 5], ((0, SMALL - TAPS - 5), (0, 0)))
    small_m = jnp.pad(whole[TAPS + 5 :], ((0, SMALL - TAPS - 5), (0, 0)))

    tiles = ring_order([a[ROWS:] for a in arrived], x).astype(F32)
    in_share = tiles[:, :INNER].reshape(BLOCK, HIDDEN_PART)
    in_mom = tiles[:, INNER:].reshape(BLOCK, HIDDEN_PART)
    half = (jnp.arange(HIDDEN_PART) // BLOCK) == y

    def bias_rows(v):
        row = jnp.where(half, jnp.concatenate([v, v]), 0.0)[None]
        return jnp.pad(row, ((0, 15), (0, 0)))

    weights = jnp.concatenate([w_out[0], in_share, bias_rows(b_in[0])], axis=0)
    moments = jnp.concatenate([mom_out[0], in_mom, bias_rows(mom_bin[0])], axis=0)

    step_images = [arrived, None]
    step_cots = [[cots[0]] + [shift(cots[0], k) for k in range(1, RING)], None]
    later = jnp.concatenate([photos[1], cots[1]], axis=0)
    ahead = [later] + [shift(later, k) for k in range(1, RING)]
    step_images[1] = ahead
    step_cots[1] = ahead

    features = None
    for step in range(STEPS):
        last = step == STEPS - 1
        own = weights.astype(BF16)
        other = swap(own)
        normed, scaled, spread = front(step_images[step], small)
        bias = (weights[2 * BLOCK] + other[2 * BLOCK].astype(F32))[None]
        outs = mlp(last, y_scalar, normed, own, other, bias, step_cots[step], small)
        g_own, g_send, dnormed, aux = outs[:4]
        g_other = swap(g_send)
        d_small = back(step_images[step], scaled, spread, dnormed, small, aux)
        if last:
            parts = [outs[4]] + [shift(outs[4 + k], RING - k) for k in range(1, RING)]
            total = sum(p.astype(F32) for p in parts) + small[TAPS + 3]
            features = (photos[step].astype(F32) + small[TAPS + 4] * total).astype(BF16)
        moments = MOMENTUM * moments + (g_own + g_other.astype(F32))
        weights = weights - RATE * moments
        theirs = passed_along(weights.astype(BF16), 2**step)
        weights = 0.5 * (weights + theirs.astype(F32))
        both = (d_small.astype(F32) + swap(d_small).astype(F32)).astype(BF16)
        rest = [shift(both, k) for k in range(1, RING)]
        grad = both.astype(F32) + sum(r.astype(F32) for r in rest)
        small_m = MOMENTUM * small_m + grad
        small = small - RATE * small_m
        if last:
            small = lax.dynamic_slice(small, (0, member * INNER), (SMALL, INNER))
        small = 0.5 * (small + passed_along(small, 2**step))

    new_bin = lax.dynamic_slice_in_dim(weights[2 * BLOCK], y * BLOCK, BLOCK, 0)
    share = weights[BLOCK : 2 * BLOCK]

    def rows_for(k):
        return lax.dynamic_slice_in_dim(share, ((x + k) % RING) * INNER, INNER, 0)

    back_tiles = [rows_for(0)] + [shift(rows_for(k), k) for k in range(1, RING)]
    new_in = ring_order(back_tiles, x).reshape(RING, INNER, PAIR, BLOCK)
    new_in = new_in.transpose(1, 2, 0, 3).reshape(INNER, PAIR * RING * BLOCK)
    return (
        small[:TAPS][None],
        small[TAPS : TAPS + 5][None],
        new_in[None],
        new_bin[None],
        weights[:BLOCK][None],
        features.reshape(1, 1, HEIGHT, WIDTH, CHANNELS),
    )


def solution(mesh):
    return jax.shard_map(
        per_device,
        mesh=mesh,
        in_specs=(
            P(None, "peer", "grp", None, None, None),
            P(None, "peer", "grp", None, None, None),
            P("peer", None, "grp"),
            P("peer", None, "grp"),
            P("peer", "grp", None),
            P("peer", "grp"),
            P("peer", "grp", None),
            P("peer", None, "grp"),
            P("peer", None, "grp"),
            P("peer", "grp", None),
            P("peer", "grp"),
            P("peer", "grp", None),
        ),
        out_specs=(
            P("peer", None, "grp"),
            P("peer", None, "grp"),
            P("peer", "grp", None),
            P("peer", "grp"),
            P("peer", "grp", None),
            P("peer", "grp", None, None, None),
        ),
        check_vma=False,
    )
```

```python
import functools

import jax
import jax.numpy as jnp
from jax import lax
from jax.experimental import pallas as pl
from jax.experimental.pallas import tpu as pltpu
from jax.sharding import PartitionSpec as P


STEPS = 2
EPS = 1e-06
MOMENTUM = 0.9
RATE = 0.0005
SQRT_HALF = 0.7071067811865476
INV_ROOT_TWO_PI = 0.3989422804014327


RING = 4
PAIR = 2
HEIGHT, WIDTH, CHANNELS = 8, 32, 384
ROWS = HEIGHT * WIDTH
HIDDEN_PART = 384
BLOCK = 192
INNER = 48
TAPS = 49
PACKED = 2 * BLOCK + 16
SMALL = 56
LANES = 128
LIMIT = 9 * 2**20

F32 = jnp.float32
BF16 = jnp.bfloat16
VMEM = pl.BlockSpec(memory_space=pltpu.VMEM)
SMEM = pl.BlockSpec(memory_space=pltpu.SMEM)


def shift(block, k):
    route = [
        (y * RING + x, y * RING + (x + k) % RING) for y in range(PAIR) for x in range(RING)
    ]
    return lax.ppermute(block, "grp", route)


def swap(block):
    route = [(y * RING + x, (1 - y) * RING + x) for y in range(PAIR) for x in range(RING)]
    return lax.ppermute(block, "grp", route)


def pair_along(block, distance, flip):
    peers, members = lax.axis_size("peer"), PAIR * RING
    route = [
        (
            ((r - distance) % peers) * members + ((1 - y) if flip else y) * RING + x,
            r * members + y * RING + x,
        )
        for r in range(peers)
        for y in range(PAIR)
        for x in range(RING)
    ]
    return lax.ppermute(block, ("peer", "grp"), route)


def passed_along(block, distance):
    count = lax.axis_size("peer")
    return lax.ppermute(block, "peer", [((i - distance) % count, i) for i in range(count)])


def ring_order(slots, x):
    a, b, c, d = slots
    return lax.dynamic_slice_in_dim(jnp.stack([d, c, b, a, d, c, b]), RING - 1 - x, RING, 0)


def fill_padded(refs, pad):
    for k, ref in enumerate(refs):
        rows = pl.ds(k * HEIGHT, HEIGHT)
        pad[rows, 0:8, :] = jnp.zeros((HEIGHT, 8, CHANNELS), F32)
        pad[rows, 8 : 8 + WIDTH, :] = (
            ref[0:ROWS, :].astype(F32).reshape(HEIGHT, WIDTH, CHANNELS)
        )
        pad[rows, 8 + WIDTH : 16 + WIDTH, :] = jnp.zeros((HEIGHT, 8, CHANNELS), F32)


def fill_shifted(pad, base, lanes, shifted):
    for j in range(7):
        for h in range(HEIGHT):
            shifted[j * HEIGHT + h] = pad[base + h, 5 + j : 5 + j + WIDTH, lanes]


def front_kernel(i0, i1, i2, i3, small, normed, scaled, spread, pad, conv, shifted):
    fill_padded((i0, i1, i2, i3), pad)

    def tile(t, carry):
        image = t // 3
        lanes = pl.ds(pl.multiple_of((t % 3) * LANES, LANES), LANES)
        base = image * HEIGHT
        bias = small[TAPS : TAPS + 1, lanes]
        fill_shifted(pad, base, lanes, shifted)
        for wt in range(WIDTH // 8):
            acc = [jnp.broadcast_to(bias, (8, LANES)) for _ in range(HEIGHT)]
            for j in range(7):
                at = slice(8 * wt, 8 * wt + 8)
                src = [shifted[j * HEIGHT + h, at, :] for h in range(HEIGHT)]
                for i in range(7):
                    tap = small[7 * i + j : 7 * i + j + 1, lanes]
                    for h in range(HEIGHT):
                        s = h + i - 3
                        if 0 <= s < HEIGHT:
                            acc[h] = acc[h] + tap * src[s]
            for h in range(HEIGHT):
                conv[(base + h) * 4 + wt, :, lanes] = acc[h]
        return carry

    lax.fori_loop(0, RING * 3, tile, 0)
    gain = small[TAPS + 1 : TAPS + 2, :]
    offset = small[TAPS + 2 : TAPS + 3, :]

    def norm(c, carry):
        v = conv[pl.ds(c * 8, 8), :, :].reshape(64, CHANNELS)
        rows = pl.ds(pl.multiple_of(c * 64, 64), 64)
        center = v - jnp.sum(v, axis=-1, keepdims=True) * (1.0 / CHANNELS)
        var = jnp.sum(center * center, axis=-1, keepdims=True) * (1.0 / CHANNELS)
        inv = lax.rsqrt(var + EPS)
        sc = center * inv
        scaled[rows, :] = sc
        spread[rows, :] = jnp.broadcast_to(inv, (64, LANES))
        normed[rows, :] = (sc * gain + offset).astype(BF16)
        return carry

    lax.fori_loop(0, RING * ROWS // 64, norm, 0)


def front(images, small):
    total = RING * ROWS
    return pl.pallas_call(
        front_kernel,
        out_shape=(
            jax.ShapeDtypeStruct((total, CHANNELS), BF16),
            jax.ShapeDtypeStruct((total, CHANNELS), F32),
            jax.ShapeDtypeStruct((total, LANES), F32),
        ),
        in_specs=[VMEM] * 5,
        out_specs=(VMEM,) * 3,
        scratch_shapes=[
            pltpu.VMEM((RING * HEIGHT, WIDTH + 16, CHANNELS), F32),
            pltpu.VMEM((RING * HEIGHT * 4, 8, CHANNELS), F32),
            pltpu.VMEM((7 * HEIGHT, WIDTH, LANES), F32),
        ],
        cost_estimate=pl.CostEstimate(flops=10**9, transcendentals=0, bytes_accessed=30 * 10**6),
        compiler_params=pltpu.CompilerParams(vmem_limit_bytes=LIMIT),
        name="front",
    )(*images, small)


def contract(a, b, da, db):
    return lax.dot_general(a, b, (((da,), (db,)), ((), ())), preferred_element_type=F32)


def mlp_kernel(
    last, y_ref, normed, own, other, b_ref, c0, c1, c2, c3, small, *refs
):
    g_own, g_send, dnormed, aux = refs[:4]
    partial = refs[4:8] if last else ()
    w_in, w_out, acc_out, acc_in = refs[-4:]
    y = y_ref[0]
    mine = pl.ds(pl.multiple_of(y * BLOCK, 64), BLOCK)
    theirs = pl.ds(pl.multiple_of((1 - y) * BLOCK, 64), BLOCK)
    w_out[mine, :] = own[0:BLOCK, :]
    w_out[theirs, :] = other[0:BLOCK, :]
    w_in[mine, :] = own[BLOCK : 2 * BLOCK, :]
    w_in[theirs, :] = other[BLOCK : 2 * BLOCK, :]
    bias = b_ref[...]
    b_out = small[TAPS + 3 : TAPS + 4, :]
    scale = small[TAPS + 4 : TAPS + 5, :]
    c_sum = jnp.zeros((1, CHANNELS), F32)
    g_bin = jnp.zeros((1, HIDDEN_PART), F32)
    for k, c_ref in enumerate((c0, c1, c2, c3)):
        rows = slice(k * ROWS, (k + 1) * ROWS)
        nrm = normed[rows, :]
        cot = c_ref[c_ref.shape[0] - ROWS :, :]
        wide = cot.astype(F32)
        pre = contract(nrm, w_in[...], 1, 0) + bias
        phi = 0.5 * (1.0 + lax.erf(pre * SQRT_HALF))
        hidden = (pre * phi).astype(BF16)
        slope = phi + pre * jnp.exp(-0.5 * pre * pre) * INV_ROOT_TWO_PI
        dmlp = (wide * scale).astype(BF16)
        dpre = (contract(dmlp, w_out[...], 1, 1) * slope).astype(BF16)
        dnormed[rows, :] = contract(dpre, w_in[...], 1, 1)
        go = contract(hidden, cot, 0, 0)
        gi = contract(nrm, dpre, 0, 0)
        if k == 0:
            acc_out[...] = go
            acc_in[...] = gi
        else:
            acc_out[...] += go
            acc_in[...] += gi
        c_sum = c_sum + jnp.sum(wide, axis=0, keepdims=True)
        g_bin = g_bin + jnp.sum(dpre.astype(F32), axis=0, keepdims=True)
        if last:
            partial[k][...] = contract(hidden, w_out[...], 1, 0).astype(BF16)
    share = 1.0 / RING
    scale_grad = jnp.sum(w_out[...].astype(F32) * acc_out[...], axis=0, keepdims=True)
    aux[0:1, :] = share * (scale * c_sum)
    aux[1:2, :] = scale_grad + share * (b_out * c_sum)
    g_own[0:BLOCK, :] = acc_out[mine, :] * scale
    g_send[0:BLOCK, :] = (acc_out[theirs, :] * scale).astype(BF16)
    g_own[BLOCK : 2 * BLOCK, :] = acc_in[mine, :]
    g_send[BLOCK : 2 * BLOCK, :] = acc_in[theirs, :].astype(BF16)
    first = lax.broadcasted_iota(jnp.int32, (16, HIDDEN_PART), 0) == 0
    half = (lax.broadcasted_iota(jnp.int32, (16, HIDDEN_PART), 1) >= BLOCK).astype(jnp.int32)
    block = jnp.broadcast_to(g_bin, (16, HIDDEN_PART))
    zero = jnp.zeros_like(block)
    g_own[2 * BLOCK :, :] = jnp.where(first & (half == y), block, zero)
    g_send[2 * BLOCK :, :] = jnp.where(first & (half != y), block, zero).astype(BF16)


def mlp(last, y, normed, own, other, bias, cots, small):
    total = RING * ROWS
    shapes = [
        jax.ShapeDtypeStruct((PACKED, CHANNELS), F32),
        pltpu.HBM((PACKED, CHANNELS), BF16),
        jax.ShapeDtypeStruct((total, CHANNELS), F32),
        jax.ShapeDtypeStruct((8, CHANNELS), F32),
    ]
    if last:
        shapes += [pltpu.HBM((ROWS, CHANNELS), BF16)] * RING
    return pl.pallas_call(
        functools.partial(mlp_kernel, last),
        out_shape=tuple(shapes),
        in_specs=[SMEM] + [VMEM] * 9,
        out_specs=(VMEM,) * len(shapes),
        scratch_shapes=[
            pltpu.VMEM((CHANNELS, HIDDEN_PART), BF16),
            pltpu.VMEM((HIDDEN_PART, CHANNELS), BF16),
            pltpu.VMEM((HIDDEN_PART, CHANNELS), F32),
            pltpu.VMEM((CHANNELS, HIDDEN_PART), F32),
        ],
        cost_estimate=pl.CostEstimate(
            flops=2 * 10**9, transcendentals=10**6, bytes_accessed=20 * 10**6
        ),
        compiler_params=pltpu.CompilerParams(vmem_limit_bytes=LIMIT),
        name="mlp",
    )(y, normed, own, other, bias, *cots, small)


def back_kernel(start, count, final, *refs):
    photos, refs = refs[:count], refs[count:]
    scaled, spread, dnormed, small, extra, out = refs[:6]
    pad, dconv, taps, rows_out, shifted = refs[6:]
    fill_padded(photos, pad)
    gain = small[TAPS + 1 : TAPS + 2, :]
    zero = jnp.zeros((8, CHANNELS), F32)

    def norm(c, sums):
        bias_sum, gain_sum, shift_sum = sums
        rows = pl.ds(pl.multiple_of(start * ROWS + c * 64, 64), 64)
        sc = scaled[rows, :]
        dn = dnormed[rows, :]
        inv = spread[rows, 0:1]
        ds = dn * gain
        mean = jnp.sum(ds, axis=-1, keepdims=True) * (1.0 / CHANNELS)
        along = jnp.sum(ds * sc, axis=-1, keepdims=True) * (1.0 / CHANNELS)
        dc = (inv * (ds - mean - sc * along)).reshape(8, 8, CHANNELS)
        dconv[pl.ds(c * 8, 8), :, :] = dc
        return (
            bias_sum + jnp.sum(dc, axis=0),
            gain_sum + jnp.sum((dn * sc).reshape(8, 8, CHANNELS), axis=0),
            shift_sum + jnp.sum(dn.reshape(8, 8, CHANNELS), axis=0),
        )

    sums = lax.fori_loop(0, count * ROWS // 64, norm, (zero, zero, zero))
    taps[...] = jnp.zeros_like(taps)

    def tile(t, carry):
        image = t // 3
        lanes = pl.ds(pl.multiple_of((t % 3) * LANES, LANES), LANES)
        base = image * HEIGHT
        fill_shifted(pad, base, lanes, shifted)
        for j in range(7):
            acc = [taps[7 * i + j, :, lanes] for i in range(7)]
            for wt in range(WIDTH // 8):
                at = slice(8 * wt, 8 * wt + 8)
                src = [shifted[j * HEIGHT + h, at, :] for h in range(HEIGHT)]
                grad = [dconv[(base + h) * 4 + wt, :, lanes] for h in range(HEIGHT)]
                for i in range(7):
                    for h in range(HEIGHT):
                        s = h + i - 3
                        if 0 <= s < HEIGHT:
                            acc[i] = acc[i] + grad[h] * src[s]
            for i in range(7):
                taps[7 * i + j, :, lanes] = acc[i]
        return carry

    lax.fori_loop(0, count * 3, tile, 0)
    rows_out[0:TAPS, :] = jnp.sum(taps[...], axis=1)
    for r, value in enumerate(sums):
        rows_out[TAPS + r : TAPS + r + 1, :] = jnp.sum(value, axis=0, keepdims=True)
    rows_out[TAPS + 3 : SMALL, :] = jnp.zeros((SMALL - TAPS - 3, CHANNELS), F32)
    if start == 0:
        rows_out[TAPS + 3 : TAPS + 5, :] = extra[0:2, :]
        total = rows_out[...]
    else:
        total = rows_out[...] + extra[...]
    out[...] = total.astype(BF16) if final else total


def back(start, final, photos, scaled, spread, dnormed, small, extra):
    count = len(photos)
    return pl.pallas_call(
        functools.partial(back_kernel, start, count, final),
        out_shape=jax.ShapeDtypeStruct((SMALL, CHANNELS), BF16 if final else F32),
        in_specs=[VMEM] * (count + 5),
        out_specs=VMEM,
        scratch_shapes=[
            pltpu.VMEM((count * HEIGHT, WIDTH + 16, CHANNELS), F32),
            pltpu.VMEM((count * HEIGHT * 4, 8, CHANNELS), F32),
            pltpu.VMEM((TAPS, 8, CHANNELS), F32),
            pltpu.VMEM((SMALL, CHANNELS), F32),
            pltpu.VMEM((7 * HEIGHT, WIDTH, LANES), F32),
        ],
        cost_estimate=pl.CostEstimate(
            flops=10**9, transcendentals=0, bytes_accessed=count * 8 * 10**6
        ),
        compiler_params=pltpu.CompilerParams(vmem_limit_bytes=LIMIT),
        name="back",
    )(*photos, scaled, spread, dnormed, small, extra)


def per_device(
    images,
    cotangent,
    dw_kernel,
    chan_vec,
    w_in,
    b_in,
    w_out,
    mom_kernel,
    mom_chan,
    mom_in,
    mom_bin,
    mom_out,
):
    member = lax.axis_index("grp")
    y, x = member // RING, member % RING
    y_scalar = y.astype(jnp.int32).reshape(1)
    photos = [images[s, 0, 0].reshape(ROWS, CHANNELS) for s in range(STEPS)]
    cots = [cotangent[s, 0, 0].reshape(ROWS, CHANNELS) for s in range(STEPS)]

    tiny = jnp.concatenate(
        [
            jnp.concatenate([dw_kernel[0], chan_vec[0]], axis=0),
            jnp.concatenate([mom_kernel[0], mom_chan[0]], axis=0),
        ],
        axis=1,
    )
    from_pair = swap(tiny)
    couple = jnp.concatenate(
        [jnp.where(y == 0, tiny, from_pair), jnp.where(y == 0, from_pair, tiny)], axis=1
    )
    couple = jnp.pad(couple, ((0, SMALL - TAPS - 5), (0, 0)))
    couple_high = lax.reduce_precision(couple, 8, 7)
    couple_low = couple - couple_high
    couple_rows = jnp.concatenate([couple_high, couple_low], axis=1).astype(BF16)

    low = jnp.concatenate([w_in[0], mom_in[0]], axis=0).astype(BF16)

    def columns(k):
        at = ((x + k) % RING) * BLOCK
        left = lax.dynamic_slice_in_dim(low, at, BLOCK, 1)
        right = lax.dynamic_slice_in_dim(low, at + RING * BLOCK, BLOCK, 1)
        return jnp.concatenate([left, right], axis=1)

    packs = [
        jnp.concatenate([photos[0], columns(k), couple_rows], axis=0) for k in range(1, RING)
    ]
    came = [shift(packs[k - 1], k) for k in range(1, RING)]
    arrived = [photos[0]] + came
    couples = [couple_rows] + [c[ROWS + 2 * INNER :] for c in came]
    whole = ring_order(couples, x).astype(F32)
    whole = (whole[:, :, : 4 * INNER] + whole[:, :, 4 * INNER :]).reshape(
        RING, SMALL, PAIR, 2, INNER
    )
    whole = whole.transpose(3, 1, 2, 0, 4).reshape(2, SMALL, CHANNELS)
    small, small_m = whole[0], whole[1]

    tiles = ring_order([columns(0)] + [c[ROWS : ROWS + 2 * INNER] for c in came], x)
    tiles = tiles.astype(F32)
    in_share = tiles[:, :INNER].reshape(BLOCK, HIDDEN_PART)
    in_mom = tiles[:, INNER:].reshape(BLOCK, HIDDEN_PART)
    half = (jnp.arange(HIDDEN_PART) // BLOCK) == y

    def bias_rows(v):
        row = jnp.where(half, jnp.concatenate([v, v]), 0.0)[None]
        return jnp.pad(row, ((0, 15), (0, 0)))

    weights = jnp.concatenate([w_out[0], in_share, bias_rows(b_in[0])], axis=0)
    moments = jnp.concatenate([mom_out[0], in_mom, bias_rows(mom_bin[0])], axis=0)

    step_images = [arrived, None]
    step_cots = [[cots[0]] + [shift(cots[0], k) for k in range(1, RING)], None]
    later = jnp.concatenate([photos[1], cots[1]], axis=0)
    ahead = [later] + [shift(later, k) for k in range(1, RING)]
    step_images[1] = ahead
    step_cots[1] = ahead

    def columns_of(v, device):
        return lax.dynamic_slice(v, (0, device * INNER), (SMALL, INNER))

    features = None
    for step in range(STEPS):
        last = step == STEPS - 1
        base = small - (RATE * MOMENTUM) * small_m
        if last:
            base = columns_of(base, member)
        base_mean = 0.5 * (base + passed_along(base, 2**step))
        own = weights.astype(BF16)
        other = swap(own)
        normed, scaled, spread = front(step_images[step], small)
        bias = (weights[2 * BLOCK] + other[2 * BLOCK].astype(F32))[None]
        outs = mlp(last, y_scalar, normed, own, other, bias, step_cots[step], small)
        g_own, g_send, dnormed, aux = outs[:4]
        g_other = swap(g_send)
        saved = (scaled, spread, dnormed, small)
        shown = step_images[step]
        if last:
            early = back(0, False, shown[:2], *saved, aux)
            d_small = back(2, True, shown[2:], *saved, early)
        else:
            d_small = back(0, True, shown, *saved, aux)
        if last:
            parts = [outs[4]] + [shift(outs[4 + k], RING - k) for k in range(1, RING)]
            total = sum(p.astype(F32) for p in parts) + small[TAPS + 3]
            features = (photos[step].astype(F32) + small[TAPS + 4] * total).astype(BF16)
        moments = MOMENTUM * moments + (g_own + g_other.astype(F32))
        weights = weights - RATE * moments
        theirs = passed_along(weights.astype(BF16), 2**step)
        weights = 0.5 * (weights + theirs.astype(F32))
        rest = [shift(d_small, k) for k in range(1, RING)]
        half_sum = d_small.astype(F32) + sum(r.astype(F32) for r in rest)
        mine = theirs = half_sum.astype(BF16)
        if last:
            mine, theirs = columns_of(mine, member), columns_of(theirs, (1 - y) * RING + x)
        near = swap(theirs).astype(F32)
        far_own = pair_along(mine, 2**step, False).astype(F32)
        far_pair = pair_along(theirs, 2**step, True).astype(F32)
        grad = mine.astype(F32) + near
        small = base_mean - (0.5 * RATE) * (grad + (far_own + far_pair))
        small_m = MOMENTUM * small_m + grad if not last else None

    new_bin = lax.dynamic_slice_in_dim(weights[2 * BLOCK], y * BLOCK, BLOCK, 0)
    share = weights[BLOCK : 2 * BLOCK]

    def rows_for(k):
        return lax.dynamic_slice_in_dim(share, ((x + k) % RING) * INNER, INNER, 0)

    back_tiles = [rows_for(0)] + [shift(rows_for(k), k) for k in range(1, RING)]
    new_in = ring_order(back_tiles, x).reshape(RING, INNER, PAIR, BLOCK)
    new_in = new_in.transpose(1, 2, 0, 3).reshape(INNER, PAIR * RING * BLOCK)
    return (
        small[:TAPS][None],
        small[TAPS : TAPS + 5][None],
        new_in[None],
        new_bin[None],
        weights[:BLOCK][None],
        features.reshape(1, 1, HEIGHT, WIDTH, CHANNELS),
    )


def solution(mesh):
    return jax.shard_map(
        per_device,
        mesh=mesh,
        in_specs=(
            P(None, "peer", "grp", None, None, None),
            P(None, "peer", "grp", None, None, None),
            P("peer", None, "grp"),
            P("peer", None, "grp"),
            P("peer", "grp", None),
            P("peer", "grp"),
            P("peer", "grp", None),
            P("peer", None, "grp"),
            P("peer", None, "grp"),
            P("peer", "grp", None),
            P("peer", "grp"),
            P("peer", "grp", None),
        ),
        out_specs=(
            P("peer", None, "grp"),
            P("peer", None, "grp"),
            P("peer", "grp", None),
            P("peer", "grp"),
            P("peer", "grp", None),
            P("peer", "grp", None, None, None),
        ),
        check_vma=False,
    )
```

```python
import functools

import jax
import jax.numpy as jnp
from jax import lax
from jax.experimental import pallas as pl
from jax.experimental.pallas import tpu as pltpu
from jax.sharding import PartitionSpec as P


STEPS = 2
EPS = 1e-06
MOMENTUM = 0.9
RATE = 0.0005
SQRT_HALF = 0.7071067811865476
INV_ROOT_TWO_PI = 0.3989422804014327


RING = 4
PAIR = 2
HEIGHT, WIDTH, CHANNELS = 8, 32, 384
ROWS = HEIGHT * WIDTH
HIDDEN_PART = 384
BLOCK = 192
INNER = 48
TAPS = 49
PACKED = 2 * BLOCK + 16
SMALL = 56
LANES = 128
LIMIT = 9 * 2**20

F32 = jnp.float32
BF16 = jnp.bfloat16
VMEM = pl.BlockSpec(memory_space=pltpu.VMEM)
SMEM = pl.BlockSpec(memory_space=pltpu.SMEM)


def shift(block, k):
    route = [
        (y * RING + x, y * RING + (x + k) % RING) for y in range(PAIR) for x in range(RING)
    ]
    return lax.ppermute(block, "grp", route)


def swap(block):
    route = [(y * RING + x, (1 - y) * RING + x) for y in range(PAIR) for x in range(RING)]
    return lax.ppermute(block, "grp", route)


def pair_along(block, distance, flip):
    peers, members = lax.axis_size("peer"), PAIR * RING
    route = [
        (
            ((r - distance) % peers) * members + ((1 - y) if flip else y) * RING + x,
            r * members + y * RING + x,
        )
        for r in range(peers)
        for y in range(PAIR)
        for x in range(RING)
    ]
    return lax.ppermute(block, ("peer", "grp"), route)


def passed_along(block, distance):
    count = lax.axis_size("peer")
    return lax.ppermute(block, "peer", [((i - distance) % count, i) for i in range(count)])


def ring_order(slots, x):
    a, b, c, d = slots
    return lax.dynamic_slice_in_dim(jnp.stack([d, c, b, a, d, c, b]), RING - 1 - x, RING, 0)


def fill_padded(refs, pad):
    for k, ref in enumerate(refs):
        rows = pl.ds(k * HEIGHT, HEIGHT)
        pad[rows, 0:8, :] = jnp.zeros((HEIGHT, 8, CHANNELS), F32)
        pad[rows, 8 : 8 + WIDTH, :] = (
            ref[0:ROWS, :].astype(F32).reshape(HEIGHT, WIDTH, CHANNELS)
        )
        pad[rows, 8 + WIDTH : 16 + WIDTH, :] = jnp.zeros((HEIGHT, 8, CHANNELS), F32)


def fill_shifted(pad, base, lanes, shifted):
    for j in range(7):
        for h in range(HEIGHT):
            shifted[j * HEIGHT + h] = pad[base + h, 5 + j : 5 + j + WIDTH, lanes]


def front_kernel(i0, i1, i2, i3, small, normed, scaled, spread, pad, conv, shifted):
    fill_padded((i0, i1, i2, i3), pad)

    def tile(t, carry):
        image = t // 3
        lanes = pl.ds(pl.multiple_of((t % 3) * LANES, LANES), LANES)
        base = image * HEIGHT
        bias = small[TAPS : TAPS + 1, lanes]
        fill_shifted(pad, base, lanes, shifted)
        for wt in range(WIDTH // 8):
            acc = [jnp.broadcast_to(bias, (8, LANES)) for _ in range(HEIGHT)]
            for j in range(7):
                at = slice(8 * wt, 8 * wt + 8)
                src = [shifted[j * HEIGHT + h, at, :] for h in range(HEIGHT)]
                for i in range(7):
                    tap = small[7 * i + j : 7 * i + j + 1, lanes]
                    for h in range(HEIGHT):
                        s = h + i - 3
                        if 0 <= s < HEIGHT:
                            acc[h] = acc[h] + tap * src[s]
            for h in range(HEIGHT):
                conv[(base + h) * 4 + wt, :, lanes] = acc[h]
        return carry

    lax.fori_loop(0, RING * 3, tile, 0)
    gain = small[TAPS + 1 : TAPS + 2, :]
    offset = small[TAPS + 2 : TAPS + 3, :]

    def norm(c, carry):
        v = conv[pl.ds(c * 8, 8), :, :].reshape(64, CHANNELS)
        rows = pl.ds(pl.multiple_of(c * 64, 64), 64)
        center = v - jnp.sum(v, axis=-1, keepdims=True) * (1.0 / CHANNELS)
        var = jnp.sum(center * center, axis=-1, keepdims=True) * (1.0 / CHANNELS)
        inv = lax.rsqrt(var + EPS)
        sc = center * inv
        scaled[rows, :] = sc
        spread[rows, :] = jnp.broadcast_to(inv, (64, LANES))
        normed[rows, :] = (sc * gain + offset).astype(BF16)
        return carry

    lax.fori_loop(0, RING * ROWS // 64, norm, 0)


def front(images, small):
    total = RING * ROWS
    return pl.pallas_call(
        front_kernel,
        out_shape=(
            jax.ShapeDtypeStruct((total, CHANNELS), BF16),
            jax.ShapeDtypeStruct((total, CHANNELS), F32),
            jax.ShapeDtypeStruct((total, LANES), F32),
        ),
        in_specs=[VMEM] * 5,
        out_specs=(VMEM,) * 3,
        scratch_shapes=[
            pltpu.VMEM((RING * HEIGHT, WIDTH + 16, CHANNELS), F32),
            pltpu.VMEM((RING * HEIGHT * 4, 8, CHANNELS), F32),
            pltpu.VMEM((7 * HEIGHT, WIDTH, LANES), F32),
        ],
        cost_estimate=pl.CostEstimate(flops=10**9, transcendentals=0, bytes_accessed=30 * 10**6),
        compiler_params=pltpu.CompilerParams(vmem_limit_bytes=LIMIT),
        name="front",
    )(*images, small)


def contract(a, b, da, db):
    return lax.dot_general(a, b, (((da,), (db,)), ((), ())), preferred_element_type=F32)


def mlp_kernel(
    last, y_ref, normed, own, other, b_ref, c0, c1, c2, c3, small, *refs
):
    g_own, g_send, dnormed, aux = refs[:4]
    partial = refs[4:8] if last else ()
    w_in, w_out, acc_out, acc_in, cots = refs[-5:]
    y = y_ref[0]
    mine = pl.ds(pl.multiple_of(y * BLOCK, 64), BLOCK)
    theirs = pl.ds(pl.multiple_of((1 - y) * BLOCK, 64), BLOCK)
    w_out[mine, :] = own[0:BLOCK, :]
    w_out[theirs, :] = other[0:BLOCK, :]
    w_in[mine, :] = own[BLOCK : 2 * BLOCK, :]
    w_in[theirs, :] = other[BLOCK : 2 * BLOCK, :]
    bias = b_ref[...]
    b_out = small[TAPS + 3 : TAPS + 4, :]
    scale = small[TAPS + 4 : TAPS + 5, :]
    top = c0.shape[0] - ROWS
    for k, c_ref in enumerate((c0, c1, c2, c3)):
        cots[k] = c_ref[top:, :]
    acc_out[...] = jnp.zeros_like(acc_out)
    acc_in[...] = jnp.zeros_like(acc_in)

    def image(k, sums):
        c_sum, g_bin = sums
        rows = pl.ds(pl.multiple_of(k * ROWS, ROWS), ROWS)
        nrm = normed[rows, :]
        cot = cots[k]
        wide = cot.astype(F32)
        pre = contract(nrm, w_in[...], 1, 0) + bias
        phi = 0.5 * (1.0 + lax.erf(pre * SQRT_HALF))
        hidden = (pre * phi).astype(BF16)
        slope = phi + pre * jnp.exp(-0.5 * pre * pre) * INV_ROOT_TWO_PI
        dmlp = (wide * scale).astype(BF16)
        dpre = (contract(dmlp, w_out[...], 1, 1) * slope).astype(BF16)
        dnormed[rows, :] = contract(dpre, w_in[...], 1, 1)
        acc_out[...] += contract(hidden, cot, 0, 0)
        acc_in[...] += contract(nrm, dpre, 0, 0)
        if last:
            product = contract(hidden, w_out[...], 1, 0).astype(BF16)
            for n in range(RING):

                @pl.when(k == n)
                def _():
                    partial[n][...] = product

        return (
            c_sum + jnp.sum(wide, axis=0, keepdims=True),
            g_bin + jnp.sum(dpre.astype(F32), axis=0, keepdims=True),
        )

    zero_row = jnp.zeros((1, CHANNELS), F32)
    c_sum, g_bin = lax.fori_loop(0, RING, image, (zero_row, zero_row))
    share = 1.0 / RING
    scale_grad = jnp.sum(w_out[...].astype(F32) * acc_out[...], axis=0, keepdims=True)
    aux[0:1, :] = share * (scale * c_sum)
    aux[1:2, :] = scale_grad + share * (b_out * c_sum)
    g_own[0:BLOCK, :] = acc_out[mine, :] * scale
    g_send[0:BLOCK, :] = (acc_out[theirs, :] * scale).astype(BF16)
    g_own[BLOCK : 2 * BLOCK, :] = acc_in[mine, :]
    g_send[BLOCK : 2 * BLOCK, :] = acc_in[theirs, :].astype(BF16)
    first = lax.broadcasted_iota(jnp.int32, (16, HIDDEN_PART), 0) == 0
    half = (lax.broadcasted_iota(jnp.int32, (16, HIDDEN_PART), 1) >= BLOCK).astype(jnp.int32)
    block = jnp.broadcast_to(g_bin, (16, HIDDEN_PART))
    zero = jnp.zeros_like(block)
    g_own[2 * BLOCK :, :] = jnp.where(first & (half == y), block, zero)
    g_send[2 * BLOCK :, :] = jnp.where(first & (half != y), block, zero).astype(BF16)


def mlp(last, y, normed, own, other, bias, cots, small):
    total = RING * ROWS
    shapes = [
        jax.ShapeDtypeStruct((PACKED, CHANNELS), F32),
        pltpu.HBM((PACKED, CHANNELS), BF16),
        jax.ShapeDtypeStruct((total, CHANNELS), F32),
        jax.ShapeDtypeStruct((8, CHANNELS), F32),
    ]
    if last:
        shapes += [pltpu.HBM((ROWS, CHANNELS), BF16)] * RING
    return pl.pallas_call(
        functools.partial(mlp_kernel, last),
        out_shape=tuple(shapes),
        in_specs=[SMEM] + [VMEM] * 9,
        out_specs=(VMEM,) * len(shapes),
        scratch_shapes=[
            pltpu.VMEM((CHANNELS, HIDDEN_PART), BF16),
            pltpu.VMEM((HIDDEN_PART, CHANNELS), BF16),
            pltpu.VMEM((HIDDEN_PART, CHANNELS), F32),
            pltpu.VMEM((CHANNELS, HIDDEN_PART), F32),
            pltpu.VMEM((RING, ROWS, CHANNELS), BF16),
        ],
        cost_estimate=pl.CostEstimate(
            flops=2 * 10**9, transcendentals=10**6, bytes_accessed=20 * 10**6
        ),
        compiler_params=pltpu.CompilerParams(vmem_limit_bytes=LIMIT),
        name="mlp",
    )(y, normed, own, other, bias, *cots, small)


def back_kernel(start, count, final, *refs):
    photos, refs = refs[:count], refs[count:]
    scaled, spread, dnormed, small, extra, out = refs[:6]
    pad, dconv, taps, rows_out, shifted = refs[6:]
    fill_padded(photos, pad)
    gain = small[TAPS + 1 : TAPS + 2, :]
    zero = jnp.zeros((8, CHANNELS), F32)

    def norm(c, sums):
        bias_sum, gain_sum, shift_sum = sums
        rows = pl.ds(pl.multiple_of(start * ROWS + c * 64, 64), 64)
        sc = scaled[rows, :]
        dn = dnormed[rows, :]
        inv = spread[rows, 0:1]
        ds = dn * gain
        mean = jnp.sum(ds, axis=-1, keepdims=True) * (1.0 / CHANNELS)
        along = jnp.sum(ds * sc, axis=-1, keepdims=True) * (1.0 / CHANNELS)
        dc = (inv * (ds - mean - sc * along)).reshape(8, 8, CHANNELS)
        dconv[pl.ds(c * 8, 8), :, :] = dc
        return (
            bias_sum + jnp.sum(dc, axis=0),
            gain_sum + jnp.sum((dn * sc).reshape(8, 8, CHANNELS), axis=0),
            shift_sum + jnp.sum(dn.reshape(8, 8, CHANNELS), axis=0),
        )

    sums = lax.fori_loop(0, count * ROWS // 64, norm, (zero, zero, zero))
    taps[...] = jnp.zeros_like(taps)

    def tile(t, carry):
        image = t // 3
        lanes = pl.ds(pl.multiple_of((t % 3) * LANES, LANES), LANES)
        base = image * HEIGHT
        fill_shifted(pad, base, lanes, shifted)
        for j in range(7):
            acc = [taps[7 * i + j, :, lanes] for i in range(7)]
            for wt in range(WIDTH // 8):
                at = slice(8 * wt, 8 * wt + 8)
                src = [shifted[j * HEIGHT + h, at, :] for h in range(HEIGHT)]
                grad = [dconv[(base + h) * 4 + wt, :, lanes] for h in range(HEIGHT)]
                for i in range(7):
                    for h in range(HEIGHT):
                        s = h + i - 3
                        if 0 <= s < HEIGHT:
                            acc[i] = acc[i] + grad[h] * src[s]
            for i in range(7):
                taps[7 * i + j, :, lanes] = acc[i]
        return carry

    lax.fori_loop(0, count * 3, tile, 0)
    rows_out[0:TAPS, :] = jnp.sum(taps[...], axis=1)
    for r, value in enumerate(sums):
        rows_out[TAPS + r : TAPS + r + 1, :] = jnp.sum(value, axis=0, keepdims=True)
    rows_out[TAPS + 3 : SMALL, :] = jnp.zeros((SMALL - TAPS - 3, CHANNELS), F32)
    if start == 0:
        rows_out[TAPS + 3 : TAPS + 5, :] = extra[0:2, :]
        total = rows_out[...]
    else:
        total = rows_out[...] + extra[...]
    out[...] = total.astype(BF16) if final else total


def back(start, final, photos, scaled, spread, dnormed, small, extra):
    count = len(photos)
    return pl.pallas_call(
        functools.partial(back_kernel, start, count, final),
        out_shape=jax.ShapeDtypeStruct((SMALL, CHANNELS), BF16 if final else F32),
        in_specs=[VMEM] * (count + 5),
        out_specs=VMEM,
        scratch_shapes=[
            pltpu.VMEM((count * HEIGHT, WIDTH + 16, CHANNELS), F32),
            pltpu.VMEM((count * HEIGHT * 4, 8, CHANNELS), F32),
            pltpu.VMEM((TAPS, 8, CHANNELS), F32),
            pltpu.VMEM((SMALL, CHANNELS), F32),
            pltpu.VMEM((7 * HEIGHT, WIDTH, LANES), F32),
        ],
        cost_estimate=pl.CostEstimate(
            flops=10**9, transcendentals=0, bytes_accessed=count * 8 * 10**6
        ),
        compiler_params=pltpu.CompilerParams(vmem_limit_bytes=LIMIT),
        name="back",
    )(*photos, scaled, spread, dnormed, small, extra)


def per_device(
    images,
    cotangent,
    dw_kernel,
    chan_vec,
    w_in,
    b_in,
    w_out,
    mom_kernel,
    mom_chan,
    mom_in,
    mom_bin,
    mom_out,
):
    member = lax.axis_index("grp")
    y, x = member // RING, member % RING
    y_scalar = y.astype(jnp.int32).reshape(1)
    photos = [images[s, 0, 0].reshape(ROWS, CHANNELS) for s in range(STEPS)]
    cots = [cotangent[s, 0, 0].reshape(ROWS, CHANNELS) for s in range(STEPS)]

    tiny = jnp.concatenate(
        [
            jnp.concatenate([dw_kernel[0], chan_vec[0]], axis=0),
            jnp.concatenate([mom_kernel[0], mom_chan[0]], axis=0),
        ],
        axis=1,
    )
    from_pair = swap(tiny)
    couple = jnp.concatenate(
        [jnp.where(y == 0, tiny, from_pair), jnp.where(y == 0, from_pair, tiny)], axis=1
    )
    couple = jnp.pad(couple, ((0, SMALL - TAPS - 5), (0, 0)))
    couple_high = lax.reduce_precision(couple, 8, 7)
    couple_low = couple - couple_high
    couple_rows = jnp.concatenate([couple_high, couple_low], axis=1).astype(BF16)

    low = jnp.concatenate([w_in[0], mom_in[0]], axis=0).astype(BF16)

    def columns(k):
        at = ((x + k) % RING) * BLOCK
        left = lax.dynamic_slice_in_dim(low, at, BLOCK, 1)
        right = lax.dynamic_slice_in_dim(low, at + RING * BLOCK, BLOCK, 1)
        return jnp.concatenate([left, right], axis=1)

    packs = [
        jnp.concatenate([photos[0], columns(k), couple_rows], axis=0) for k in range(1, RING)
    ]
    came = [shift(packs[k - 1], k) for k in range(1, RING)]
    arrived = [photos[0]] + came
    couples = [couple_rows] + [c[ROWS + 2 * INNER :] for c in came]
    whole = ring_order(couples, x).astype(F32)
    whole = (whole[:, :, : 4 * INNER] + whole[:, :, 4 * INNER :]).reshape(
        RING, SMALL, PAIR, 2, INNER
    )
    whole = whole.transpose(3, 1, 2, 0, 4).reshape(2, SMALL, CHANNELS)
    small, small_m = whole[0], whole[1]

    tiles = ring_order([columns(0)] + [c[ROWS : ROWS + 2 * INNER] for c in came], x)
    tiles = tiles.astype(F32)
    in_share = tiles[:, :INNER].reshape(BLOCK, HIDDEN_PART)
    in_mom = tiles[:, INNER:].reshape(BLOCK, HIDDEN_PART)
    half = (jnp.arange(HIDDEN_PART) // BLOCK) == y

    def bias_rows(v):
        row = jnp.where(half, jnp.concatenate([v, v]), 0.0)[None]
        return jnp.pad(row, ((0, 15), (0, 0)))

    weights = jnp.concatenate([w_out[0], in_share, bias_rows(b_in[0])], axis=0)
    moments = jnp.concatenate([mom_out[0], in_mom, bias_rows(mom_bin[0])], axis=0)

    step_images = [arrived, None]
    step_cots = [[cots[0]] + [shift(cots[0], k) for k in range(1, RING)], None]
    later = jnp.concatenate([photos[1], cots[1]], axis=0)
    ahead = [later] + [shift(later, k) for k in range(1, RING)]
    step_images[1] = ahead
    step_cots[1] = ahead

    def columns_of(v, device):
        return lax.dynamic_slice(v, (0, device * INNER), (SMALL, INNER))

    features = None
    for step in range(STEPS):
        last = step == STEPS - 1
        base = small - (RATE * MOMENTUM) * small_m
        if last:
            base = columns_of(base, member)
        own = weights.astype(BF16)
        other = swap(own)
        normed, scaled, spread = front(step_images[step], small)
        bias = (weights[2 * BLOCK] + other[2 * BLOCK].astype(F32))[None]
        outs = mlp(last, y_scalar, normed, own, other, bias, step_cots[step], small)
        g_own, g_send, dnormed, aux = outs[:4]
        g_other = swap(g_send)
        saved = (scaled, spread, dnormed, small)
        shown = step_images[step]
        if last:
            early = back(0, False, shown[:2], *saved, aux)
            d_small = back(2, True, shown[2:], *saved, early)
        else:
            d_small = back(0, True, shown, *saved, aux)
        if last:
            parts = [outs[4]] + [shift(outs[4 + k], RING - k) for k in range(1, RING)]
            total = sum(p.astype(F32) for p in parts) + small[TAPS + 3]
            features = (photos[step].astype(F32) + small[TAPS + 4] * total).astype(BF16)
        moments = MOMENTUM * moments + (g_own + g_other.astype(F32))
        weights = weights - RATE * moments
        theirs = passed_along(weights.astype(BF16), 2**step)
        weights = 0.5 * (weights + theirs.astype(F32))
        rest = [shift(d_small, k) for k in range(1, RING)]
        half_sum = d_small.astype(F32) + sum(r.astype(F32) for r in rest)
        mine = theirs = half_sum.astype(BF16)
        if last:
            mine, theirs = columns_of(mine, member), columns_of(theirs, (1 - y) * RING + x)
        near = swap(theirs).astype(F32)
        part_step = base - RATE * mine.astype(F32)
        far_own = pair_along(part_step, 2**step, False)
        far_pair = pair_along(theirs, 2**step, True).astype(F32)
        grad = mine.astype(F32) + near
        small = 0.5 * ((base - RATE * grad) + (far_own - RATE * far_pair))
        small_m = MOMENTUM * small_m + grad if not last else None

    new_bin = lax.dynamic_slice_in_dim(weights[2 * BLOCK], y * BLOCK, BLOCK, 0)
    share = weights[BLOCK : 2 * BLOCK]

    def rows_for(k):
        return lax.dynamic_slice_in_dim(share, ((x + k) % RING) * INNER, INNER, 0)

    back_tiles = [rows_for(0)] + [shift(rows_for(k), k) for k in range(1, RING)]
    new_in = ring_order(back_tiles, x).reshape(RING, INNER, PAIR, BLOCK)
    new_in = new_in.transpose(1, 2, 0, 3).reshape(INNER, PAIR * RING * BLOCK)
    return (
        small[:TAPS][None],
        small[TAPS : TAPS + 5][None],
        new_in[None],
        new_bin[None],
        weights[:BLOCK][None],
        features.reshape(1, 1, HEIGHT, WIDTH, CHANNELS),
    )


def solution(mesh):
    return jax.shard_map(
        per_device,
        mesh=mesh,
        in_specs=(
            P(None, "peer", "grp", None, None, None),
            P(None, "peer", "grp", None, None, None),
            P("peer", None, "grp"),
            P("peer", None, "grp"),
            P("peer", "grp", None),
            P("peer", "grp"),
            P("peer", "grp", None),
            P("peer", None, "grp"),
            P("peer", None, "grp"),
            P("peer", "grp", None),
            P("peer", "grp"),
            P("peer", "grp", None),
        ),
        out_specs=(
            P("peer", None, "grp"),
            P("peer", None, "grp"),
            P("peer", "grp", None),
            P("peer", "grp"),
            P("peer", "grp", None),
            P("peer", "grp", None, None, None),
        ),
        check_vma=False,
    )
```

```python
import functools

import jax
import jax.numpy as jnp
from jax import lax
from jax.experimental import pallas as pl
from jax.experimental.pallas import tpu as pltpu
from jax.sharding import PartitionSpec as P


STEPS = 2
EPS = 1e-06
MOMENTUM = 0.9
RATE = 0.0005
SQRT_HALF = 0.7071067811865476
INV_ROOT_TWO_PI = 0.3989422804014327


RING = 4
PAIR = 2
HEIGHT, WIDTH, CHANNELS = 8, 32, 384
ROWS = HEIGHT * WIDTH
HIDDEN_PART = 384
BLOCK = 192
INNER = 48
TAPS = 49
PACKED = 2 * BLOCK + 16
SMALL = 56
LANES = 128
LIMIT = 9 * 2**20

F32 = jnp.float32
BF16 = jnp.bfloat16
VMEM = pl.BlockSpec(memory_space=pltpu.VMEM)
SMEM = pl.BlockSpec(memory_space=pltpu.SMEM)


def shift(block, k):
    route = [
        (y * RING + x, y * RING + (x + k) % RING) for y in range(PAIR) for x in range(RING)
    ]
    return lax.ppermute(block, "grp", route)


def swap(block):
    route = [(y * RING + x, (1 - y) * RING + x) for y in range(PAIR) for x in range(RING)]
    return lax.ppermute(block, "grp", route)


def pair_along(block, distance, flip):
    peers, members = lax.axis_size("peer"), PAIR * RING
    route = [
        (
            ((r - distance) % peers) * members + ((1 - y) if flip else y) * RING + x,
            r * members + y * RING + x,
        )
        for r in range(peers)
        for y in range(PAIR)
        for x in range(RING)
    ]
    return lax.ppermute(block, ("peer", "grp"), route)


def passed_along(block, distance):
    count = lax.axis_size("peer")
    return lax.ppermute(block, "peer", [((i - distance) % count, i) for i in range(count)])


def ring_order(slots, x):
    a, b, c, d = slots
    return lax.dynamic_slice_in_dim(jnp.stack([d, c, b, a, d, c, b]), RING - 1 - x, RING, 0)


def fill_padded(refs, pad):
    for k, ref in enumerate(refs):
        rows = pl.ds(k * HEIGHT, HEIGHT)
        pad[rows, 0:8, :] = jnp.zeros((HEIGHT, 8, CHANNELS), F32)
        pad[rows, 8 : 8 + WIDTH, :] = (
            ref[0:ROWS, :].astype(F32).reshape(HEIGHT, WIDTH, CHANNELS)
        )
        pad[rows, 8 + WIDTH : 16 + WIDTH, :] = jnp.zeros((HEIGHT, 8, CHANNELS), F32)


def fill_shifted(pad, base, lanes, shifted):
    for j in range(7):
        for h in range(HEIGHT):
            shifted[j * HEIGHT + h] = pad[base + h, 5 + j : 5 + j + WIDTH, lanes]


def front_kernel(i0, i1, i2, i3, small, normed, scaled, spread, pad, conv, shifted):
    fill_padded((i0, i1, i2, i3), pad)

    def tile(t, carry):
        image = t // 3
        lanes = pl.ds(pl.multiple_of((t % 3) * LANES, LANES), LANES)
        base = image * HEIGHT
        bias = small[TAPS : TAPS + 1, lanes]
        fill_shifted(pad, base, lanes, shifted)
        for wt in range(WIDTH // 8):
            acc = [jnp.broadcast_to(bias, (8, LANES)) for _ in range(HEIGHT)]
            for j in range(7):
                at = slice(8 * wt, 8 * wt + 8)
                src = [shifted[j * HEIGHT + h, at, :] for h in range(HEIGHT)]
                for i in range(7):
                    tap = small[7 * i + j : 7 * i + j + 1, lanes]
                    for h in range(HEIGHT):
                        s = h + i - 3
                        if 0 <= s < HEIGHT:
                            acc[h] = acc[h] + tap * src[s]
            for h in range(HEIGHT):
                conv[(base + h) * 4 + wt, :, lanes] = acc[h]
        return carry

    lax.fori_loop(0, RING * 3, tile, 0)
    gain = small[TAPS + 1 : TAPS + 2, :]
    offset = small[TAPS + 2 : TAPS + 3, :]

    def norm(c, carry):
        v = conv[pl.ds(c * 8, 8), :, :].reshape(64, CHANNELS)
        rows = pl.ds(pl.multiple_of(c * 64, 64), 64)
        center = v - jnp.sum(v, axis=-1, keepdims=True) * (1.0 / CHANNELS)
        var = jnp.sum(center * center, axis=-1, keepdims=True) * (1.0 / CHANNELS)
        inv = lax.rsqrt(var + EPS)
        sc = center * inv
        scaled[rows, :] = sc
        spread[rows, :] = jnp.broadcast_to(inv, (64, LANES))
        normed[rows, :] = (sc * gain + offset).astype(BF16)
        return carry

    lax.fori_loop(0, RING * ROWS // 64, norm, 0)


def front(images, small):
    total = RING * ROWS
    return pl.pallas_call(
        front_kernel,
        out_shape=(
            jax.ShapeDtypeStruct((total, CHANNELS), BF16),
            jax.ShapeDtypeStruct((total, CHANNELS), F32),
            jax.ShapeDtypeStruct((total, LANES), F32),
        ),
        in_specs=[VMEM] * 5,
        out_specs=(VMEM,) * 3,
        scratch_shapes=[
            pltpu.VMEM((RING * HEIGHT, WIDTH + 16, CHANNELS), F32),
            pltpu.VMEM((RING * HEIGHT * 4, 8, CHANNELS), F32),
            pltpu.VMEM((7 * HEIGHT, WIDTH, LANES), F32),
        ],
        cost_estimate=pl.CostEstimate(flops=10**9, transcendentals=0, bytes_accessed=30 * 10**6),
        compiler_params=pltpu.CompilerParams(vmem_limit_bytes=LIMIT),
        name="front",
    )(*images, small)


def contract(a, b, da, db):
    return lax.dot_general(a, b, (((da,), (db,)), ((), ())), preferred_element_type=F32)


def mlp_kernel(
    last, y_ref, normed, own, other, b_ref, c0, c1, c2, c3, small, *refs
):
    g_own, g_send, dnormed, aux = refs[:4]
    partial = refs[4:8] if last else ()
    w_in, w_out, acc_out, acc_in, cots = refs[-5:]
    y = y_ref[0]
    mine = pl.ds(pl.multiple_of(y * BLOCK, 64), BLOCK)
    theirs = pl.ds(pl.multiple_of((1 - y) * BLOCK, 64), BLOCK)
    w_out[mine, :] = own[0:BLOCK, :]
    w_out[theirs, :] = other[0:BLOCK, :]
    w_in[mine, :] = own[BLOCK : 2 * BLOCK, :]
    w_in[theirs, :] = other[BLOCK : 2 * BLOCK, :]
    bias = b_ref[...]
    b_out = small[TAPS + 3 : TAPS + 4, :]
    scale = small[TAPS + 4 : TAPS + 5, :]
    top = c0.shape[0] - ROWS
    for k, c_ref in enumerate((c0, c1, c2, c3)):
        cots[k] = c_ref[top:, :]
    acc_out[...] = jnp.zeros_like(acc_out)
    acc_in[...] = jnp.zeros_like(acc_in)

    def image(k, sums):
        c_sum, g_bin = sums
        rows = pl.ds(pl.multiple_of(k * ROWS, ROWS), ROWS)
        nrm = normed[rows, :]
        cot = cots[k]
        wide = cot.astype(F32)
        pre = contract(nrm, w_in[...], 1, 0) + bias
        phi = 0.5 * (1.0 + lax.erf(pre * SQRT_HALF))
        hidden = (pre * phi).astype(BF16)
        slope = phi + pre * jnp.exp(-0.5 * pre * pre) * INV_ROOT_TWO_PI
        dmlp = (wide * scale).astype(BF16)
        dpre = (contract(dmlp, w_out[...], 1, 1) * slope).astype(BF16)
        dnormed[rows, :] = contract(dpre, w_in[...], 1, 1)
        acc_out[...] += contract(hidden, cot, 0, 0)
        acc_in[...] += contract(nrm, dpre, 0, 0)
        if last:
            product = contract(hidden, w_out[...], 1, 0).astype(BF16)
            for n in range(RING):

                @pl.when(k == n)
                def _():
                    partial[n][...] = product

        return (
            c_sum + jnp.sum(wide, axis=0, keepdims=True),
            g_bin + jnp.sum(dpre.astype(F32), axis=0, keepdims=True),
        )

    zero_row = jnp.zeros((1, CHANNELS), F32)
    c_sum, g_bin = lax.fori_loop(0, RING, image, (zero_row, zero_row))
    share = 1.0 / RING
    scale_grad = jnp.sum(w_out[...].astype(F32) * acc_out[...], axis=0, keepdims=True)
    aux[0:1, :] = share * (scale * c_sum)
    aux[1:2, :] = scale_grad + share * (b_out * c_sum)
    g_own[0:BLOCK, :] = acc_out[mine, :] * scale
    g_send[0:BLOCK, :] = (acc_out[theirs, :] * scale).astype(BF16)
    g_own[BLOCK : 2 * BLOCK, :] = acc_in[mine, :]
    g_send[BLOCK : 2 * BLOCK, :] = acc_in[theirs, :].astype(BF16)
    first = lax.broadcasted_iota(jnp.int32, (16, HIDDEN_PART), 0) == 0
    half = (lax.broadcasted_iota(jnp.int32, (16, HIDDEN_PART), 1) >= BLOCK).astype(jnp.int32)
    block = jnp.broadcast_to(g_bin, (16, HIDDEN_PART))
    zero = jnp.zeros_like(block)
    g_own[2 * BLOCK :, :] = jnp.where(first & (half == y), block, zero)
    g_send[2 * BLOCK :, :] = jnp.where(first & (half != y), block, zero).astype(BF16)


def mlp(last, y, normed, own, other, bias, cots, small):
    total = RING * ROWS
    shapes = [
        jax.ShapeDtypeStruct((PACKED, CHANNELS), F32),
        pltpu.HBM((PACKED, CHANNELS), BF16),
        jax.ShapeDtypeStruct((total, CHANNELS), F32),
        jax.ShapeDtypeStruct((8, CHANNELS), F32),
    ]
    if last:
        shapes += [pltpu.HBM((ROWS, CHANNELS), BF16)] * RING
    return pl.pallas_call(
        functools.partial(mlp_kernel, last),
        out_shape=tuple(shapes),
        in_specs=[SMEM] + [VMEM] * 9,
        out_specs=(VMEM,) * len(shapes),
        scratch_shapes=[
            pltpu.VMEM((CHANNELS, HIDDEN_PART), BF16),
            pltpu.VMEM((HIDDEN_PART, CHANNELS), BF16),
            pltpu.VMEM((HIDDEN_PART, CHANNELS), F32),
            pltpu.VMEM((CHANNELS, HIDDEN_PART), F32),
            pltpu.VMEM((RING, ROWS, CHANNELS), BF16),
        ],
        cost_estimate=pl.CostEstimate(
            flops=2 * 10**9, transcendentals=10**6, bytes_accessed=20 * 10**6
        ),
        compiler_params=pltpu.CompilerParams(vmem_limit_bytes=LIMIT),
        name="mlp",
    )(y, normed, own, other, bias, *cots, small)


def back_kernel(start, count, final, *refs):
    photos, refs = refs[:count], refs[count:]
    scaled, spread, dnormed, small, extra, out = refs[:6]
    pad, dconv, taps, rows_out, shifted = refs[6:]
    fill_padded(photos, pad)
    gain = small[TAPS + 1 : TAPS + 2, :]
    zero = jnp.zeros((8, CHANNELS), F32)

    def norm(c, sums):
        bias_sum, gain_sum, shift_sum = sums
        rows = pl.ds(pl.multiple_of(start * ROWS + c * 64, 64), 64)
        sc = scaled[rows, :]
        dn = dnormed[rows, :]
        inv = spread[rows, 0:1]
        ds = dn * gain
        mean = jnp.sum(ds, axis=-1, keepdims=True) * (1.0 / CHANNELS)
        along = jnp.sum(ds * sc, axis=-1, keepdims=True) * (1.0 / CHANNELS)
        dc = (inv * (ds - mean - sc * along)).reshape(8, 8, CHANNELS)
        dconv[pl.ds(c * 8, 8), :, :] = dc
        return (
            bias_sum + jnp.sum(dc, axis=0),
            gain_sum + jnp.sum((dn * sc).reshape(8, 8, CHANNELS), axis=0),
            shift_sum + jnp.sum(dn.reshape(8, 8, CHANNELS), axis=0),
        )

    sums = lax.fori_loop(0, count * ROWS // 64, norm, (zero, zero, zero))
    taps[...] = jnp.zeros_like(taps)

    def tile(t, carry):
        image = t // 3
        lanes = pl.ds(pl.multiple_of((t % 3) * LANES, LANES), LANES)
        base = image * HEIGHT
        fill_shifted(pad, base, lanes, shifted)
        for j in range(7):
            acc = [taps[7 * i + j, :, lanes] for i in range(7)]
            for wt in range(WIDTH // 8):
                at = slice(8 * wt, 8 * wt + 8)
                src = [shifted[j * HEIGHT + h, at, :] for h in range(HEIGHT)]
                grad = [dconv[(base + h) * 4 + wt, :, lanes] for h in range(HEIGHT)]
                for i in range(7):
                    for h in range(HEIGHT):
                        s = h + i - 3
                        if 0 <= s < HEIGHT:
                            acc[i] = acc[i] + grad[h] * src[s]
            for i in range(7):
                taps[7 * i + j, :, lanes] = acc[i]
        return carry

    lax.fori_loop(0, count * 3, tile, 0)
    rows_out[0:TAPS, :] = jnp.sum(taps[...], axis=1)
    for r, value in enumerate(sums):
        rows_out[TAPS + r : TAPS + r + 1, :] = jnp.sum(value, axis=0, keepdims=True)
    rows_out[TAPS + 3 : SMALL, :] = jnp.zeros((SMALL - TAPS - 3, CHANNELS), F32)
    if start == 0:
        rows_out[TAPS + 3 : TAPS + 5, :] = extra[0:2, :]
        total = rows_out[...]
    else:
        total = rows_out[...] + extra[...]
    out[...] = total.astype(BF16) if final else total


def back(start, final, photos, scaled, spread, dnormed, small, extra):
    count = len(photos)
    return pl.pallas_call(
        functools.partial(back_kernel, start, count, final),
        out_shape=jax.ShapeDtypeStruct((SMALL, CHANNELS), BF16 if final else F32),
        in_specs=[VMEM] * (count + 5),
        out_specs=VMEM,
        scratch_shapes=[
            pltpu.VMEM((count * HEIGHT, WIDTH + 16, CHANNELS), F32),
            pltpu.VMEM((count * HEIGHT * 4, 8, CHANNELS), F32),
            pltpu.VMEM((TAPS, 8, CHANNELS), F32),
            pltpu.VMEM((SMALL, CHANNELS), F32),
            pltpu.VMEM((7 * HEIGHT, WIDTH, LANES), F32),
        ],
        cost_estimate=pl.CostEstimate(
            flops=10**9, transcendentals=0, bytes_accessed=count * 8 * 10**6
        ),
        compiler_params=pltpu.CompilerParams(vmem_limit_bytes=LIMIT),
        name="back",
    )(*photos, scaled, spread, dnormed, small, extra)


def per_device(
    images,
    cotangent,
    dw_kernel,
    chan_vec,
    w_in,
    b_in,
    w_out,
    mom_kernel,
    mom_chan,
    mom_in,
    mom_bin,
    mom_out,
):
    member = lax.axis_index("grp")
    y, x = member // RING, member % RING
    y_scalar = y.astype(jnp.int32).reshape(1)
    photos = [images[s, 0, 0].reshape(ROWS, CHANNELS) for s in range(STEPS)]
    cots = [cotangent[s, 0, 0].reshape(ROWS, CHANNELS) for s in range(STEPS)]

    tiny = jnp.concatenate(
        [
            jnp.concatenate([dw_kernel[0], chan_vec[0]], axis=0),
            jnp.concatenate([mom_kernel[0], mom_chan[0]], axis=0),
        ],
        axis=1,
    )
    from_pair = swap(tiny)
    couple = jnp.concatenate(
        [jnp.where(y == 0, tiny, from_pair), jnp.where(y == 0, from_pair, tiny)], axis=1
    )
    couple = jnp.pad(couple, ((0, SMALL - TAPS - 5), (0, 0)))
    couple_high = lax.reduce_precision(couple, 8, 7)
    couple_low = couple - couple_high
    couple_rows = jnp.concatenate([couple_high, couple_low], axis=1).astype(BF16)

    low = jnp.concatenate([w_in[0], mom_in[0]], axis=0).astype(BF16)

    def columns(k):
        at = ((x + k) % RING) * BLOCK
        left = lax.dynamic_slice_in_dim(low, at, BLOCK, 1)
        right = lax.dynamic_slice_in_dim(low, at + RING * BLOCK, BLOCK, 1)
        return jnp.concatenate([left, right], axis=1)

    packs = [
        jnp.concatenate([photos[0], columns(k), couple_rows], axis=0) for k in range(1, RING)
    ]
    came = [shift(packs[k - 1], k) for k in range(1, RING)]
    arrived = [photos[0]] + came
    couples = [couple_rows] + [c[ROWS + 2 * INNER :] for c in came]
    whole = ring_order(couples, x).astype(F32)
    whole = (whole[:, :, : 4 * INNER] + whole[:, :, 4 * INNER :]).reshape(
        RING, SMALL, PAIR, 2, INNER
    )
    whole = whole.transpose(3, 1, 2, 0, 4).reshape(2, SMALL, CHANNELS)
    small, small_m = whole[0], whole[1]

    tiles = ring_order([columns(0)] + [c[ROWS : ROWS + 2 * INNER] for c in came], x)
    tiles = tiles.astype(F32)
    in_share = tiles[:, :INNER].reshape(BLOCK, HIDDEN_PART)
    in_mom = tiles[:, INNER:].reshape(BLOCK, HIDDEN_PART)
    half = (jnp.arange(HIDDEN_PART) // BLOCK) == y

    def bias_rows(v):
        row = jnp.where(half, jnp.concatenate([v, v]), 0.0)[None]
        return jnp.pad(row, ((0, 15), (0, 0)))

    weights = jnp.concatenate([w_out[0], in_share, bias_rows(b_in[0])], axis=0)
    moments = jnp.concatenate([mom_out[0], in_mom, bias_rows(mom_bin[0])], axis=0)

    step_images = [arrived, None]
    step_cots = [[cots[0]] + [shift(cots[0], k) for k in range(1, RING)], None]
    later = jnp.concatenate([photos[1], cots[1]], axis=0)
    ahead = [later] + [shift(later, k) for k in range(1, RING)]
    step_images[1] = ahead
    step_cots[1] = ahead

    def columns_of(v, device):
        return lax.dynamic_slice(v, (0, device * INNER), (SMALL, INNER))

    features = None
    for step in range(STEPS):
        last = step == STEPS - 1
        base = small - (RATE * MOMENTUM) * small_m
        own = weights.astype(BF16)
        other = swap(own)
        normed, scaled, spread = front(step_images[step], small)
        bias = (weights[2 * BLOCK] + other[2 * BLOCK].astype(F32))[None]
        outs = mlp(last, y_scalar, normed, own, other, bias, step_cots[step], small)
        g_own, g_send, dnormed, aux = outs[:4]
        g_other = swap(g_send)
        saved = (scaled, spread, dnormed, small)
        shown = step_images[step]
        if last:
            early = back(0, False, shown[:2], *saved, aux)
            d_small = back(2, True, shown[2:], *saved, early)
        else:
            d_small = back(0, True, shown, *saved, aux)
        if last:
            parts = [outs[4]] + [shift(outs[4 + k], RING - k) for k in range(1, RING)]
            total = sum(p.astype(F32) for p in parts) + small[TAPS + 3]
            features = (photos[step].astype(F32) + small[TAPS + 4] * total).astype(BF16)
        moments = MOMENTUM * moments + (g_own + g_other.astype(F32))
        weights = weights - RATE * moments
        theirs = passed_along(weights.astype(BF16), 2**step)
        weights = 0.5 * (weights + theirs.astype(F32))
        rest = [shift(d_small, k) for k in range(1, RING)]
        half_sum = d_small.astype(F32) + sum(r.astype(F32) for r in rest)
        mine = half_sum.astype(BF16)
        near = swap(mine).astype(F32)
        part_step = base - RATE * mine.astype(F32)
        far_own = pair_along(part_step, 2**step, False)
        far_pair = pair_along(mine, 2**step, True).astype(F32)
        grad = mine.astype(F32) + near
        small = 0.5 * ((base - RATE * grad) + (far_own - RATE * far_pair))
        small_m = MOMENTUM * small_m + grad if not last else None

    small = columns_of(small, member)
    new_bin = lax.dynamic_slice_in_dim(weights[2 * BLOCK], y * BLOCK, BLOCK, 0)
    share = weights[BLOCK : 2 * BLOCK]

    def rows_for(k):
        return lax.dynamic_slice_in_dim(share, ((x + k) % RING) * INNER, INNER, 0)

    back_tiles = [rows_for(0)] + [shift(rows_for(k), k) for k in range(1, RING)]
    new_in = ring_order(back_tiles, x).reshape(RING, INNER, PAIR, BLOCK)
    new_in = new_in.transpose(1, 2, 0, 3).reshape(INNER, PAIR * RING * BLOCK)
    return (
        small[:TAPS][None],
        small[TAPS : TAPS + 5][None],
        new_in[None],
        new_bin[None],
        weights[:BLOCK][None],
        features.reshape(1, 1, HEIGHT, WIDTH, CHANNELS),
    )


def solution(mesh):
    return jax.shard_map(
        per_device,
        mesh=mesh,
        in_specs=(
            P(None, "peer", "grp", None, None, None),
            P(None, "peer", "grp", None, None, None),
            P("peer", None, "grp"),
            P("peer", None, "grp"),
            P("peer", "grp", None),
            P("peer", "grp"),
            P("peer", "grp", None),
            P("peer", None, "grp"),
            P("peer", None, "grp"),
            P("peer", "grp", None),
            P("peer", "grp"),
            P("peer", "grp", None),
        ),
        out_specs=(
            P("peer", None, "grp"),
            P("peer", None, "grp"),
            P("peer", "grp", None),
            P("peer", "grp"),
            P("peer", "grp", None),
            P("peer", "grp", None, None, None),
        ),
        check_vma=False,
    )
```
